32 devices in a mesh: paths: 2 (over x), qa: 8 (over z, y), qb: 2 (over core).
Axes of the slice: x: 2, y: 2, z: 4, core: 2. Of those that a mesh axis runs over, the one named last changes fastest.
Arguments:
- state: float32 [2, 4194304], P(None, ('paths', 'qa', 'qb')), parts along dimension 1, may hold values from -6 to 6
- gate_terms: float32 [18, 2, 2, 128, 128], replicated, may hold values from -0.375 to 0.375
- path_bits: int32 [36], P('paths'), parts along dimension 0, may hold values from 0 to 1
Outputs:
- final_state: float32 [2, 4194304], P(None, ('paths', 'qa', 'qb')), parts along dimension 1
The draws below stay inside these ranges and needn't reach their ends.
There are 2 independent parts, one for each index of `paths`. The reference program is written for one: setup_inputs(seed, part) draws one part's arguments, and reference() takes and returns one part's arrays. A program takes and returns all parts, laid end to end along the dimension named above; an argument that names none is the same for every part. Nothing has to cross between parts.
All inputs are finite; a program needn't handle non-finite values.
Results may differ from the reference program's by a relative error of at most 0.00013.
Values sent between devices are 32-bit elements; how exact they have to be, the bound alone decides.
A program may use at most 64 MiB of HBM per device.

```python
import jax
import jax.numpy as jnp
from jax import lax

LOCAL = 17
GQ = 7
GDIM = 128
TERMS = 2
NGATES = 18
AMPS = 2097152
N_QA = 8


def plant(entries, stream_key, least, largest):
    longest = entries.shape.index(max(entries.shape))
    spots = []
    for shift in (0, 1):
        where = [jax.random.randint(jax.random.fold_in(stream_key, axis), (), 0, length) for axis, length in enumerate(entries.shape)]
        where[longest] = (where[longest] + shift) % entries.shape[longest]
        spots.append(tuple(where))
    return entries.at[spots[0]].set(least).at[spots[1]].set(largest)


def level_of(rng, dims, cuts, least, largest):
    level = 1.0
    for axis_at, blocks in cuts:
        steps = jax.random.uniform(jax.random.fold_in(jax.random.fold_in(rng, 6), axis_at), (blocks,), jnp.float32, least / len(cuts), largest / len(cuts))
        level = level * jnp.repeat(jnp.exp(steps), dims[axis_at] // blocks).reshape((-1,) + (1,) * (len(dims) - 1 - axis_at))
    return level


def normal_values(key, extent, spread, limit, split=(), kind=jnp.bfloat16):
    array = spread * jax.random.normal(key, extent, jnp.float32)
    if split:
        array = array * level_of(key, extent, split, -0.22, 0.18)
    return jnp.clip(array, -limit, limit).astype(kind)


def setup_inputs(seed: int = 0, part: int = 0) -> dict:
    key_list = jax.random.split(jax.random.key(seed), 4)
    part_keys = jax.random.split(jax.random.fold_in(key_list[3], part), 4)
    return {
        "state": normal_values(part_keys[0], (2, AMPS), 1.0, 6.0, ((1, 16),), jnp.float32),
        "gate_terms": normal_values(key_list[1], (NGATES, TERMS, 2, GDIM, GDIM), (2 * GDIM) ** -0.5, 0.375, (), jnp.float32),
        "path_bits": plant(jax.random.randint(part_keys[2], (NGATES,), 0, TERMS), jax.random.fold_in(part_keys[2], 1), 0, TERMS - 1).astype(jnp.int32),
    }


def window_offsets(span, gate_bits):
    return [0, span, gate_bits, span - 1, gate_bits + 1, span - 2]


def swap_bits(amplitudes, lower, upper, how_many):
    total_bits = amplitudes.shape[1].bit_length() - 1
    shaped = amplitudes.reshape(2, 2 ** (total_bits - upper - how_many), 2 ** how_many, 2 ** (upper - lower - how_many), 2 ** how_many, 2 ** lower)
    return jnp.swapaxes(shaped, 2, 4).reshape(2, -1)


def apply_gate(amplitudes, matrix, offset):
    gate_dim = matrix.shape[-1]
    blocked = jnp.stack([jnp.stack([matrix[0], -matrix[1]]), jnp.stack([matrix[1], matrix[0]])])
    shaped = amplitudes.reshape(2, -1, gate_dim, 2 ** offset)
    result = jnp.einsum("pqrc,qhcl->phrl", blocked, shaped, precision=lax.Precision.HIGHEST)
    return result.reshape(2, -1)


def reference(state, gate_terms, path_bits):
    local_bits = LOCAL
    qa_bits = N_QA.bit_length() - 1
    outer_span = local_bits - GQ
    inner_span = local_bits - GQ - 1
    gates = gate_terms[jnp.arange(NGATES, dtype=jnp.int32), path_bits.astype(jnp.int32)]
    amplitudes = swap_bits(state, local_bits - qa_bits, local_bits + 1, qa_bits)
    for index, offset in enumerate(window_offsets(outer_span, GQ)):
        amplitudes = apply_gate(amplitudes, gates[index], offset)
    amplitudes = swap_bits(amplitudes, local_bits - 2 * qa_bits, local_bits + 1, qa_bits)
    for index, offset in enumerate(window_offsets(inner_span, GQ)):
        amplitudes = apply_gate(amplitudes, gates[6 + index], offset)
    amplitudes = swap_bits(amplitudes, local_bits - 1, local_bits, 1)
    for index, offset in enumerate(window_offsets(outer_span, GQ)):
        amplitudes = apply_gate(amplitudes, gates[12 + index], offset)
    return amplitudes
```

```python
import functools

import jax
import jax.numpy as jnp
from jax import lax
from jax.experimental import pallas as pl
from jax.experimental.pallas import tpu as pltpu
from jax.sharding import PartitionSpec as P

MESH = pl.DeviceIdType.MESH
HIGHEST = lax.Precision.HIGHEST


def window_offsets(span, gate_bits):
    return [0, span, gate_bits, span - 1, gate_bits + 1, span - 2]


def row_gates(local_bits, gate_bits):
    sections = []
    for section, drop in enumerate((0, 1, 0)):
        merged = []
        for index, offset in enumerate(window_offsets(local_bits - gate_bits - drop, gate_bits)):
            if offset == 0:
                continue
            gate = 6 * section + index
            if merged and merged[-1][0] == offset - gate_bits:
                merged[-1][1].append(gate)
            else:
                merged.append((offset - gate_bits, [gate]))
        sections.append(merged)
    return sections


def split(x):
    high = x.astype(jnp.bfloat16)
    return high, (x - high.astype(jnp.float32)).astype(jnp.bfloat16)


def kernel(n_qa, sections, x_hbm, terms_hbm, bits_ref, out_ref,
           first, other, second, terms, weights, lane_weights,
           send_one, recv_one, send_two, recv_two, local_sem):
    qa = lax.axis_index("qa")
    qb = lax.axis_index("qb")
    rows, dim = x_hbm.shape
    block = rows // n_qa
    half = rows // 2
    low = rows // 4 // n_qa // (n_qa // 2) * 2
    middle = half // (n_qa * low)

    fetch = pltpu.make_async_copy(terms_hbm, terms, local_sem.at[0])
    fetch.start()

    barrier = pltpu.get_barrier_semaphore()
    for d in range(n_qa):
        for b in range(2):
            if d or b:
                pl.semaphore_signal(
                    barrier, inc=1,
                    device_id={"qa": lax.rem(qa + d, n_qa), "qb": lax.rem(qb + b, 2)},
                    device_id_type=MESH,
                )
    pl.semaphore_wait(barrier, 2 * n_qa - 1)

    def rows_of(which):
        return pl.ds(pl.multiple_of(which * block, block), block)

    def copy_one(d):
        peer = lax.rem(qa + d, n_qa)
        return pltpu.make_async_remote_copy(
            src_ref=x_hbm.at[rows_of(peer)],
            dst_ref=first.at[rows_of(qa)],
            send_sem=send_one.at[d],
            recv_sem=recv_one.at[d],
            device_id={"qa": peer},
            device_id_type=MESH,
        )

    ones = [copy_one(d) for d in range(1, n_qa)]
    for copy in ones:
        copy.start()
    own = pltpu.make_async_copy(x_hbm.at[rows_of(qa)], first.at[rows_of(qa)], local_sem.at[1])
    own.start()

    fetch.wait()

    def blocked(re, im):
        return jnp.concatenate(
            [jnp.concatenate([re, -im], axis=1), jnp.concatenate([im, re], axis=1)], axis=0
        )

    def product(gates):
        re = terms[gates[0], bits_ref[gates[0]], 0]
        im = terms[gates[0], bits_ref[gates[0]], 1]
        for gate in gates[1:]:
            left = blocked(terms[gate, bits_ref[gate], 0], terms[gate, bits_ref[gate], 1])
            both = jnp.dot(
                left, jnp.concatenate([re, im], axis=0),
                preferred_element_type=jnp.float32, precision=HIGHEST,
            )
            re, im = both[:dim], both[dim:]
        return blocked(re, im)

    lane_high, lane_low = split(product([0, 6, 12]))
    lane_weights[0] = lane_high
    lane_weights[1] = lane_low
    slot = 0
    for section in sections:
        for _, gates in section:
            high, lower = split(product(gates))
            weights[slot, : 2 * dim] = high
            weights[slot, 2 * dim :] = lower
            slot += 1

    def lanes(which):
        base = which * block
        count = block // 2
        re = first[pl.ds(base, count, stride=2), :]
        im = first[pl.ds(base + 1, count, stride=2), :]
        high, lower = split(jnp.concatenate([re, im], axis=1))
        dims = (((1,), (1,)), ((), ()))
        dot = functools.partial(
            lax.dot_general, dimension_numbers=dims, preferred_element_type=jnp.float32
        )
        y = dot(high, lane_weights[0]) + (dot(lower, lane_weights[0]) + dot(high, lane_weights[1]))
        first[pl.ds(base, count, stride=2), :] = y[:, :dim]
        first[pl.ds(base + 1, count, stride=2), :] = y[:, dim:]

    own.wait()
    lanes(qa)
    for d in range(1, n_qa):
        ones[d - 1].wait_recv()
        lanes(lax.rem(qa + n_qa - d, n_qa))

    def apply(src, dst, slot, offset, base, count):
        stride = 2 ** (offset + 1)
        starts = [
            hi * stride * dim + 2 * lo for hi in range(count // (stride * dim)) for lo in range(2**offset)
        ]
        for pair in range(0, len(starts), 2):
            columns = []
            for start in starts[pair : pair + 2]:
                columns.append(jnp.concatenate([
                    src[pl.ds(base + start, dim, stride=stride), :],
                    src[pl.ds(base + start + 1, dim, stride=stride), :],
                ], axis=0))
            high, lower = split(jnp.concatenate(columns, axis=1))
            both = jnp.dot(weights[slot], high, preferred_element_type=jnp.float32)
            y = both[: 2 * dim] + (
                both[2 * dim :]
                + jnp.dot(weights[slot, : 2 * dim], lower, preferred_element_type=jnp.float32)
            )
            for j, start in enumerate(starts[pair : pair + 2]):
                dst[pl.ds(base + start, dim, stride=stride), :] = y[:dim, j * dim : (j + 1) * dim]
                dst[pl.ds(base + start + 1, dim, stride=stride), :] = y[dim:, j * dim : (j + 1) * dim]

    (s0, s1, s2, s3), (t0, t1, t2, t3), (u0, u1, u2, u3) = [[o for o, _ in s] for s in sections]
    apply(first, other, 0, s0, 0, rows)
    apply(other, first, 1, s1, 0, rows)

    def view(ref, b, k):
        return ref.reshape(2, middle, n_qa, low, dim).at[b, :, k]

    def copy_two(d, b):
        peer = lax.rem(qa + d, n_qa)
        to = lax.rem(qb + b, 2)
        return pltpu.make_async_remote_copy(
            src_ref=view(first, to, peer),
            dst_ref=view(second, qb, qa),
            send_sem=send_two.at[b, d],
            recv_sem=recv_two.at[b, d],
            device_id={"qa": peer, "qb": to},
            device_id_type=MESH,
        )

    twos = {}
    for b in range(2):
        base = pl.multiple_of(lax.rem(qb + b, 2) * half, half)
        apply(first, other, 2, s2, base, half)
        apply(other, first, 3, s3, base, half)
        for d in range(n_qa):
            if d or b:
                twos[b, d] = copy_two(d, b)
            else:
                twos[b, d] = pltpu.make_async_copy(
                    view(first, qb, qa), view(second, qb, qa), local_sem.at[2]
                )
            twos[b, d].start()

    for b in range(2):
        for d in range(n_qa):
            if d or b:
                twos[b, d].wait_recv()
            else:
                twos[b, d].wait()
        base = pl.multiple_of(lax.rem(qb + b, 2) * half, half)
        apply(second, other, 4, t0, base, half)
        apply(other, second, 5, t1, base, half)
        apply(second, other, 6, t2, base, half)
        apply(other, second, 7, t3, base, half)

    apply(second, other, 8, u0, 0, rows)
    apply(other, second, 9, u1, 0, rows)
    apply(second, other, 10, u2, 0, rows)
    apply(other, out_ref, 11, u3, 0, rows)

    for copy in ones:
        copy.wait_send()
    for (b, d), copy in twos.items():
        if d or b:
            copy.wait_send()


def per_device(state, gate_terms, path_bits):
    n_qa = lax.axis_size("qa")
    dim = gate_terms.shape[-1]
    gate_bits = dim.bit_length() - 1
    amps = state.shape[1]
    local_bits = amps.bit_length() - 1
    rows = 2 * amps // dim
    sections = row_gates(local_bits, gate_bits)
    count = sum(len(s) for s in sections)
    x = state.reshape(2, rows // 2, dim).transpose(1, 0, 2).reshape(rows, dim)
    y = pl.pallas_call(
        functools.partial(kernel, n_qa, sections),
        out_shape=jax.ShapeDtypeStruct((rows, dim), jnp.float32),
        in_specs=[
            pl.BlockSpec(memory_space=pl.ANY),
            pl.BlockSpec(memory_space=pl.ANY),
            pl.BlockSpec(memory_space=pltpu.SMEM),
        ],
        out_specs=pl.BlockSpec(memory_space=pltpu.VMEM),
        scratch_shapes=[
            pltpu.VMEM((rows, dim), jnp.float32),
            pltpu.VMEM((rows, dim), jnp.float32),
            pltpu.VMEM((rows, dim), jnp.float32),
            pltpu.VMEM(gate_terms.shape, jnp.float32),
            pltpu.VMEM((count, 4 * dim, 2 * dim), jnp.bfloat16),
            pltpu.VMEM((2, 2 * dim, 2 * dim), jnp.bfloat16),
            pltpu.SemaphoreType.DMA((n_qa,)),
            pltpu.SemaphoreType.DMA((n_qa,)),
            pltpu.SemaphoreType.DMA((2, n_qa)),
            pltpu.SemaphoreType.DMA((2, n_qa)),
            pltpu.SemaphoreType.DMA((3,)),
        ],
        compiler_params=pltpu.CompilerParams(
            collective_id=0, has_side_effects=True, vmem_limit_bytes=48 * 2**20
        ),
    )(x, gate_terms, path_bits)
    return y.reshape(rows // 2, 2, dim).transpose(1, 0, 2).reshape(2, amps)


def solution(mesh):
    return jax.shard_map(
        per_device,
        mesh=mesh,
        in_specs=(P(None, ("paths", "qa", "qb")), P(), P("paths")),
        out_specs=P(None, ("paths", "qa", "qb")),
        check_vma=False,
    )
```

```python
import functools

import jax
import jax.numpy as jnp
from jax import lax
from jax.experimental import pallas as pl
from jax.experimental.pallas import tpu as pltpu
from jax.sharding import PartitionSpec as P

MESH = pl.DeviceIdType.MESH
HIGHEST = lax.Precision.HIGHEST


def window_offsets(span, gate_bits):
    return [0, span, gate_bits, span - 1, gate_bits + 1, span - 2]


def row_gates(local_bits, gate_bits):
    sections = []
    for section, drop in enumerate((0, 1, 0)):
        merged = []
        for index, offset in enumerate(window_offsets(local_bits - gate_bits - drop, gate_bits)):
            if offset == 0:
                continue
            gate = 6 * section + index
            if merged and merged[-1][0] == offset - gate_bits:
                merged[-1][1].append(gate)
            else:
                merged.append((offset - gate_bits, [gate]))
        sections.append(merged)
    return sections


def split(x):
    high = x.astype(jnp.bfloat16)
    return high, (x - high.astype(jnp.float32)).astype(jnp.bfloat16)


def kernel(n_qa, sections, x_ref, terms_hbm, bits_hbm, out_ref,
           sent, first, other, second, total, terms, bits_ref, weights, lane_weights,
           send_one, recv_one, send_two, recv_two, local_sem, own_sem):
    qa = lax.axis_index("qa")
    qb = lax.axis_index("qb")
    _, rows, dim = first.shape
    lane_half = dim // 2
    block = rows // n_qa
    half = rows // 2
    low = rows // n_qa**2
    middle = half // (n_qa * low)

    fetch = pltpu.make_async_copy(terms_hbm, terms, local_sem.at[0])
    fetch.start()
    fetch_bits = pltpu.make_async_copy(bits_hbm, bits_ref, local_sem.at[1])
    fetch_bits.start()

    barrier = pltpu.get_barrier_semaphore()
    for d in range(n_qa):
        for b in range(2):
            if d or b:
                pl.semaphore_signal(
                    barrier, inc=1,
                    device_id={"qa": lax.rem(qa + d, n_qa), "qb": lax.rem(qb + b, 2)},
                    device_id_type=MESH,
                )

    def rows_of(which):
        return pl.ds(pl.multiple_of(which * block, block), block)

    def shuffle(c):
        at = slice(c * lane_half, (c + 1) * lane_half)
        for k in range(n_qa):
            re = x_ref[pl.ds(2 * k * block, block, stride=2), :]
            im = x_ref[pl.ds(2 * k * block + 1, block, stride=2), :]
            sent[c, k * block : (k + 1) * block, :] = jnp.concatenate([re[:, at], im[:, at]], axis=1)

    def copy_one(c, d):
        peer = lax.rem(qa + d, n_qa)
        src = sent.at[c, rows_of(peer)]
        dst = first.at[c, rows_of(qa)]
        if d == 0:
            return pltpu.make_async_copy(src, dst, own_sem.at[0, c])
        return pltpu.make_async_remote_copy(
            src_ref=src, dst_ref=dst, send_sem=send_one.at[c, d], recv_sem=recv_one.at[c, d],
            device_id={"qa": peer}, device_id_type=MESH,
        )

    ones = {}
    for c in range(2):
        shuffle(c)
        if c == 0:
            pl.semaphore_wait(barrier, 2 * n_qa - 1)
        for d in range(n_qa):
            ones[c, d] = copy_one(c, d)
            ones[c, d].start()

    fetch_bits.wait()
    fetch.wait()

    def product(gates):
        re = terms[gates[0], bits_ref[gates[0]], 0]
        im = terms[gates[0], bits_ref[gates[0]], 1]
        for gate in gates[1:]:
            left_re = terms[gate, bits_ref[gate], 0]
            left_im = terms[gate, bits_ref[gate], 1]
            left = jnp.concatenate([
                jnp.concatenate([left_re, -left_im], axis=1),
                jnp.concatenate([left_im, left_re], axis=1),
            ], axis=0)
            both = jnp.dot(
                left, jnp.concatenate([re, im], axis=0),
                preferred_element_type=jnp.float32, precision=HIGHEST,
            )
            re, im = both[:dim], both[dim:]
        return re, im

    slot = 0
    for section in sections:
        for _, gates in section:
            re, im = product(gates)
            high, lower = split(jnp.concatenate([re, im], axis=0))
            weights[slot, : 2 * dim, :dim] = high
            weights[slot, : 2 * dim, dim:] = high
            weights[slot, 2 * dim :, :dim] = lower
            weights[slot, 2 * dim :, dim:] = jnp.zeros_like(lower)
            slot += 1
    re, im = product([0, 6, 12])
    for c in range(2):
        at = slice(c * lane_half, (c + 1) * lane_half)
        high, lower = split(jnp.concatenate([
            jnp.concatenate([re[:, at], -im[:, at]], axis=1),
            jnp.concatenate([im[:, at], re[:, at]], axis=1),
        ], axis=0))
        lane_weights[c, :, :dim] = high
        lane_weights[c, :, dim : 2 * dim] = high
        lane_weights[c, :, 2 * dim :] = lower

    sign = jnp.where(lax.broadcasted_iota(jnp.int32, (dim, dim), 1) < lane_half, -1.0, 1.0)

    def apply(src, dst, slot, offset, base, count):
        stride = 2**offset
        starts = [hi * stride * dim + lo for hi in range(count // (stride * dim)) for lo in range(stride)]
        for pair in range(0, len(starts), 2):
            at = [
                pl.ds(base + start, dim, stride=stride) if stride > 1 else pl.ds(base + start, dim)
                for start in starts[pair : pair + 2]
            ]
            high, lower = split(jnp.concatenate([src[a, :] for a in at], axis=1))
            both = jnp.dot(
                weights[slot], jnp.concatenate([high, lower], axis=0),
                preferred_element_type=jnp.float32,
            )
            both = both[: 2 * dim] + both[2 * dim :]
            for j, a in enumerate(at):
                plain = both[:dim, j * dim : (j + 1) * dim]
                turned = both[dim:, j * dim : (j + 1) * dim]
                dst[a, :] = plain + sign * pltpu.roll(turned, lane_half, axis=1)

    (s0, s1, s2, s3), (t0, t1, t2, t3), (u0, u1, u2, u3) = [[o for o, _ in s] for s in sections]

    def view(ref, c, b, k):
        return ref.reshape(2, 2, middle, n_qa, low, dim).at[c, b, :, k]

    def copy_two(c, d, b):
        peer = lax.rem(qa + d, n_qa)
        to = lax.rem(qb + b, 2)
        src = view(first, c, to, peer)
        dst = view(second, c, qb, qa)
        if d == 0 and b == 0:
            return pltpu.make_async_copy(src, dst, own_sem.at[1, c])
        return pltpu.make_async_remote_copy(
            src_ref=src, dst_ref=dst, send_sem=send_two.at[c, b, d], recv_sem=recv_two.at[c, b, d],
            device_id={"qa": peer, "qb": to}, device_id_type=MESH,
        )

    def arrive(copy, own):
        if own:
            copy.wait()
        else:
            copy.wait_recv()

    twos = {}
    for c in range(2):
        here = first.at[c]
        for d in range(n_qa):
            arrive(ones[c, d], d == 0)
        apply(here, other, 0, s0, 0, rows)
        apply(other, here, 1, s1, 0, rows)
        for b in range(2):
            base = pl.multiple_of(lax.rem(qb + b, 2) * half, half)
            apply(here, other, 2, s2, base, half)
            apply(other, here, 3, s3, base, half)
            for d in range(n_qa):
                twos[c, d, b] = copy_two(c, d, b)
                twos[c, d, b].start()

    for c in range(2):
        here = second.at[c]
        for b in range(2):
            for d in range(n_qa):
                arrive(twos[c, d, b], d == 0 and b == 0)
            base = pl.multiple_of(lax.rem(qb + b, 2) * half, half)
            apply(here, other, 4, t0, base, half)
            apply(other, here, 5, t1, base, half)
            apply(here, other, 6, t2, base, half)
            apply(other, here, 7, t3, base, half)
        apply(here, other, 8, u0, 0, rows)
        apply(other, here, 9, u1, 0, rows)
        apply(here, other, 10, u2, 0, rows)
        apply(other, here, 11, u3, 0, rows)
        dims = (((1,), (1,)), ((), ()))
        for k in range(rows // (2 * dim)):
            at = slice(2 * k * dim, 2 * (k + 1) * dim)
            high, lower = split(here[at, :])
            y = lax.dot_general(
                jnp.concatenate([high, lower], axis=1), lane_weights[c, :, : 2 * dim], dims,
                preferred_element_type=jnp.float32,
            ) + lax.dot_general(
                high, lane_weights[c, :, 2 * dim :], dims, preferred_element_type=jnp.float32
            )
            if c == 0:
                total[at, :] = y
            else:
                y = y + total[at, :]
                out_ref[pl.ds(4 * k * dim, 2 * dim, stride=2), :] = y[:, :dim]
                out_ref[pl.ds(4 * k * dim + 1, 2 * dim, stride=2), :] = y[:, dim:]

    for (c, d), copy in ones.items():
        if d:
            copy.wait_send()
    for (c, d, b), copy in twos.items():
        if d or b:
            copy.wait_send()


def per_device(state, gate_terms, path_bits):
    n_qa = lax.axis_size("qa")
    dim = gate_terms.shape[-1]
    gate_bits = dim.bit_length() - 1
    amps = state.shape[1]
    local_bits = amps.bit_length() - 1
    rows = 2 * amps // dim
    sections = row_gates(local_bits, gate_bits)
    count = sum(len(s) for s in sections)
    x = state.reshape(2, rows // 2, dim).transpose(1, 0, 2).reshape(rows, dim)
    y = pl.pallas_call(
        functools.partial(kernel, n_qa, sections),
        out_shape=jax.ShapeDtypeStruct((rows, dim), jnp.float32),
        in_specs=[
            pl.BlockSpec(memory_space=pltpu.VMEM),
            pl.BlockSpec(memory_space=pl.ANY),
            pl.BlockSpec(memory_space=pl.ANY),
        ],
        out_specs=pl.BlockSpec(memory_space=pltpu.VMEM),
        scratch_shapes=[
            pltpu.VMEM((2, rows // 2, dim), jnp.float32),
            pltpu.VMEM((2, rows // 2, dim), jnp.float32),
            pltpu.VMEM((rows // 2, dim), jnp.float32),
            pltpu.VMEM((2, rows // 2, dim), jnp.float32),
            pltpu.VMEM((rows // 2, 2 * dim), jnp.float32),
            pltpu.VMEM(gate_terms.shape, jnp.float32),
            pltpu.SMEM(path_bits.shape, jnp.int32),
            pltpu.VMEM((count, 4 * dim, 2 * dim), jnp.bfloat16),
            pltpu.VMEM((2, 2 * dim, 3 * dim), jnp.bfloat16),
            pltpu.SemaphoreType.DMA((2, n_qa)),
            pltpu.SemaphoreType.DMA((2, n_qa)),
            pltpu.SemaphoreType.DMA((2, 2, n_qa)),
            pltpu.SemaphoreType.DMA((2, 2, n_qa)),
            pltpu.SemaphoreType.DMA((2,)),
            pltpu.SemaphoreType.DMA((2, 2)),
        ],
        compiler_params=pltpu.CompilerParams(
            collective_id=0, has_side_effects=True, vmem_limit_bytes=48 * 2**20
        ),
    )(x, gate_terms, path_bits)
    return y.reshape(rows // 2, 2, dim).transpose(1, 0, 2).reshape(2, amps)


def solution(mesh):
    return jax.shard_map(
        per_device,
        mesh=mesh,
        in_specs=(P(None, ("paths", "qa", "qb")), P(), P("paths")),
        out_specs=P(None, ("paths", "qa", "qb")),
        check_vma=False,
    )
```
